128 devices in a mesh: rep: 16 (over x, y), shard: 8 (over z, core).
Axes of the slice: x: 4, y: 4, z: 4, core: 2. Of those that a mesh axis runs over, the one named last changes fastest.
Arguments:
- sq_grad: float32 [96, 768, 768], P(None, ('rep', 'shard'))
- sq_moment: float32 [96, 768, 768], P(None, ('rep', 'shard')), may hold values from -6 to 6
- sq_weight: float32 [96, 768, 768], P(None, ('rep', 'shard')), may hold values from -0.21875 to 0.21875
- in_grad: float32 [16, 768, 3072], P(None, ('rep', 'shard'))
- in_moment: float32 [16, 768, 3072], P(None, ('rep', 'shard')), may hold values from -6 to 6
- in_weight: float32 [16, 768, 3072], P(None, ('rep', 'shard')), may hold values from -0.21875 to 0.21875
- out_grad: float32 [16, 3072, 768], P(None, ('rep', 'shard'))
- out_moment: float32 [16, 3072, 768], P(None, ('rep', 'shard')), may hold values from -6 to 6
- out_weight: float32 [16, 3072, 768], P(None, ('rep', 'shard')), may hold values from -0.109375 to 0.109375
- emb_grad: float32 [3072, 768], P(('rep', 'shard'))
- emb_moment: float32 [3072, 768], P(('rep', 'shard')), may hold values from -6 to 6
- emb_weight: float32 [3072, 768], P(('rep', 'shard')), may hold values from -0.21875 to 0.21875
Outputs:
- sq_moment_new: float32 [96, 768, 768], P(None, ('rep', 'shard'))
- sq_weight_new: float32 [96, 768, 768], P(None, ('rep', 'shard'))
- sq_direction: float32 [96, 768, 768], P(None, ('rep', 'shard'))
- in_moment_new: float32 [16, 768, 3072], P(None, ('rep', 'shard'))
- in_weight_new: float32 [16, 768, 3072], P(None, ('rep', 'shard'))
- in_direction: float32 [16, 768, 3072], P(None, ('rep', 'shard'))
- out_moment_new: float32 [16, 3072, 768], P(None, ('rep', 'shard'))
- out_weight_new: float32 [16, 3072, 768], P(None, ('rep', 'shard'))
- out_direction: float32 [16, 3072, 768], P(None, ('rep', 'shard'))
- emb_moment_new: float32 [3072, 768], P(('rep', 'shard'))
- emb_weight_new: float32 [3072, 768], P(('rep', 'shard'))
- emb_direction: float32 [3072, 768], P(('rep', 'shard'))
The draws below stay inside these ranges and needn't reach their ends.
All inputs are finite; a program needn't handle non-finite values.
Results may differ from the reference program's by a relative error of at most 0.019.
Values may be sent and summed in bfloat16 or wider, within the bound.
No kernel may reach another device: no remote copies, remote signals or barrier semaphores. Data moves between devices by JAX's collectives and lax.ppermute only.
A program may use at most 192 MiB of HBM per device.

```python
import math
import jax
import jax.numpy as jnp
from jax import lax

D = 768
FF = 3072
V = 3072
ITERS = 3
NSQ = 96
NIN = 16
NOUT = 16


def rough_field(key, shape):
    first_key, second_key, third_key = jax.random.split(key, 3)
    leading = shape[:-2]
    row_count = shape[-2]
    col_count = shape[-1]
    top_log = math.log(10.0)
    row_scale = jnp.exp(jax.random.uniform(first_key, leading + (row_count, 1), jnp.float32, 0.0, top_log))
    col_scale = jnp.exp(jax.random.uniform(second_key, leading + (1, col_count), jnp.float32, 0.0, top_log))
    base = jax.random.normal(third_key, shape, jnp.float32)
    return base * row_scale * col_scale / 10.0


def draw_sq_grad(key, part):
    return rough_field(jax.random.fold_in(key, 11), (NSQ, D, D))


def draw_in_grad(key, part):
    return rough_field(jax.random.fold_in(key, 12), (NIN, D, FF))


def draw_out_grad(key, part):
    return rough_field(jax.random.fold_in(key, 13), (NOUT, FF, D))


def draw_emb_grad(key, part):
    return rough_field(jax.random.fold_in(key, 14), (V, D))


def shard_levels(key, shape, pieces, smallest, largest):
    gain, own = 1.0, jax.random.fold_in(key, 6)
    for dim, parts in pieces:
        steps = jnp.exp(jax.random.uniform(jax.random.fold_in(own, dim), (parts,), jnp.float32, smallest / len(pieces), largest / len(pieces)))
        gain = gain * jnp.repeat(steps, shape[dim] // parts).reshape([-1 if axis == dim else 1 for axis in range(len(shape))])
    return gain


def scatter_about(rng, dims, scale, most, cuts=(), kind=jnp.bfloat16):
    loudness = shard_levels(rng, dims, cuts, -0.22, 0.18) if cuts else 1.0
    drawn = jax.random.normal(rng, dims, jnp.float32) * scale * loudness
    return jnp.minimum(jnp.maximum(drawn, -most), most).astype(kind)


def setup_inputs(seed: int = 0) -> dict:
    key_of = jax.random.split(jax.random.key(seed), 13)
    sq_grad = draw_sq_grad(jax.random.fold_in(key_of[12], 71), 0)
    sq_moment = scatter_about(key_of[1], (NSQ, D, D), 1.0, 6.0, ((1, 128),), jnp.float32)
    sq_weight = scatter_about(key_of[2], (NSQ, D, D), D ** -0.5, 0.21875, ((1, 128),), jnp.float32)
    in_grad = draw_in_grad(jax.random.fold_in(key_of[12], 71), 0)
    in_moment = scatter_about(key_of[4], (NIN, D, FF), 1.0, 6.0, ((1, 128),), jnp.float32)
    in_weight = scatter_about(key_of[5], (NIN, D, FF), D ** -0.5, 0.21875, ((1, 128),), jnp.float32)
    out_grad = draw_out_grad(jax.random.fold_in(key_of[12], 71), 0)
    out_moment = scatter_about(key_of[7], (NOUT, FF, D), 1.0, 6.0, ((1, 128),), jnp.float32)
    out_weight = scatter_about(key_of[8], (NOUT, FF, D), FF ** -0.5, 0.109375, ((1, 128),), jnp.float32)
    emb_grad = draw_emb_grad(jax.random.fold_in(key_of[12], 71), 0)
    emb_moment = scatter_about(key_of[10], (V, D), 1.0, 6.0, ((0, 128),), jnp.float32)
    emb_weight = scatter_about(key_of[11], (V, D), D ** -0.5, 0.21875, ((0, 128),), jnp.float32)
    return {"sq_grad": sq_grad, "sq_moment": sq_moment, "sq_weight": sq_weight, "in_grad": in_grad, "in_moment": in_moment, "in_weight": in_weight, "out_grad": out_grad, "out_moment": out_moment, "out_weight": out_weight, "emb_grad": emb_grad, "emb_moment": emb_moment, "emb_weight": emb_weight}


FIRST_COEF = 3.4445
SECOND_COEF = -4.775
THIRD_COEF = 2.0315
MOMENTUM_DECAY = 0.95
STEP_RATE = 0.004
WEIGHT_DECAY = 0.1
EPSILON = 1e-07

def orthogonal(advance):
    row_count = advance.shape[0]
    col_count = advance.shape[1]
    frobenius = jnp.sqrt(jnp.sum(advance * advance))
    scaled = (advance / (frobenius + EPSILON)).astype(jnp.bfloat16)
    if row_count > col_count:
        scaled = scaled.T
    for sweep in range(ITERS):
        gram_matrix = jnp.dot(scaled, scaled.T, preferred_element_type=jnp.float32).astype(jnp.bfloat16)
        square = jnp.dot(gram_matrix, gram_matrix, preferred_element_type=jnp.float32)
        polynomial = (SECOND_COEF * gram_matrix.astype(jnp.float32) + THIRD_COEF * square).astype(jnp.bfloat16)
        product = jnp.dot(polynomial, scaled, preferred_element_type=jnp.float32)
        scaled = (FIRST_COEF * scaled.astype(jnp.float32) + product).astype(jnp.bfloat16)
    if row_count > col_count:
        scaled = scaled.T
    return math.sqrt(max(row_count, col_count)) * scaled.astype(jnp.float32)

def update_group(gradient, previous, weight_stack):
    moment_new = MOMENTUM_DECAY * previous + gradient
    advance = gradient + MOMENTUM_DECAY * moment_new
    direction = lax.map(orthogonal, advance)
    weight_new = weight_stack - STEP_RATE * (direction + WEIGHT_DECAY * weight_stack)
    return (moment_new, weight_new, direction)

def reference(sq_grad, sq_moment, sq_weight, in_grad, in_moment, in_weight, out_grad, out_moment, out_weight, emb_grad, emb_moment, emb_weight):
    sq_moment_new, sq_weight_new, sq_direction = update_group(sq_grad, sq_moment, sq_weight)
    in_moment_new, in_weight_new, in_direction = update_group(in_grad, in_moment, in_weight)
    out_moment_new, out_weight_new, out_direction = update_group(out_grad, out_moment, out_weight)
    emb_moment_new, emb_weight_new, emb_direction = update_group(emb_grad[None], emb_moment[None], emb_weight[None])
    return (sq_moment_new, sq_weight_new, sq_direction, in_moment_new, in_weight_new, in_direction, out_moment_new, out_weight_new, out_direction, emb_moment_new[0], emb_weight_new[0], emb_direction[0])
```

```python
import math

import jax
import jax.numpy as jnp
from jax import lax
from jax.experimental import pallas as pl
from jax.experimental.pallas import tpu as pltpu
from jax.sharding import PartitionSpec as P

A_COEF = 3.4445
B_COEF = -4.775
C_COEF = 2.0315
MOMENTUM_DECAY = 0.95
STEP_RATE = 0.004
WEIGHT_DECAY = 0.1
EPSILON = 1e-07
AXES = ("rep", "shard")

W = 768
LANES = 1152
F32 = jnp.float32
BF16 = jnp.bfloat16

TILES = LANES // 128
COLS = W // 128


def cell(k, c):
    if k < 8:
        return k, c
    return k - 8 + 4 * (c // 3), COLS + c % 3


def lanes(c):
    return slice(128 * c, 128 * c + 128)


def advance_of(grad, moment):
    return grad + MOMENTUM_DECAY * (MOMENTUM_DECAY * moment + grad)


def vmem_limit():
    return pltpu.CompilerParams(vmem_limit_bytes=60 * 1024 * 1024)


class Plan:
    def __init__(self, squares, wides, talls, devices):
        self.squares = squares
        self.wides = wides
        self.talls = talls
        self.tall_base = 2 * wides
        self.emb_base = self.tall_base + 2 * talls
        self.sq_base = self.emb_base + 2
        self.half = squares // 2
        self.devices = devices
        assert self.sq_base + self.half <= devices
        assert self.half % 8 == 0 and wides % 8 == 0 and talls % 8 == 0


def pack(plan, sq, wide, tall, emb):
    rows = plan.devices * 8
    arrays = (sq[0], sq[1], wide[0], wide[1], tall[0], tall[1], emb[0], emb[1])

    def kernel(*refs):
        hbm = refs[:8]
        send = refs[8]
        local = refs[9:17]
        z, zb, sems, out_sems = refs[17:21]
        copies = []
        n_sem = 0

        def fetch(which, start, size):
            nonlocal n_sem
            pair = []
            for t in (2 * which, 2 * which + 1):
                if which == 2:
                    ends = hbm[t].at[:, lanes(start)], local[t].at[start]
                else:
                    at = pl.ds(start, size)
                    ends = hbm[t].at[at], local[t].at[at]
                c = pltpu.make_async_copy(*ends, sems.at[n_sem])
                n_sem += 1
                c.start()
                pair.append(c)
            return pair

        w_cp = [fetch(1, r * plan.wides, plan.wides) for r in range(6)]
        t_cp = [fetch(2, c, None) for c in range(COLS)]
        e_cp = fetch(3, 0, 24)
        s_cp = [fetch(0, r * plan.squares, plan.squares) for r in range(6)]

        def put(k, c, dest0, step, value):
            sub, j = cell(k, c)
            z[j, pl.ds(dest0 * 8 + sub, 8, stride=8 * step), :] = value

        def flush(i, start, size):
            for j in range(TILES):
                zb[pl.ds(start, size), lanes(j)] = z[j, pl.ds(start, size), :].astype(BF16)
            c = pltpu.make_async_copy(
                zb.at[pl.ds(start, size)], send.at[pl.ds(start, size)], out_sems.at[i]
            )
            c.start()
            copies.append(c)

        for r in range(6):
            for c in w_cp[r]:
                c.wait()
            for g in range(plan.wides // 8):
                at = pl.ds(r * plan.wides + 8 * g, 8)
                for h in range(2):
                    for ab in range(2):
                        lane = (2 * h + ab) * W
                        v = advance_of(
                            local[2][at, lane : lane + W], local[3][at, lane : lane + W]
                        )
                        for c in range(COLS):
                            put(6 * ab + r, c, 16 * g + h, 2, v[:, lanes(c)])
        flush(0, 0, plan.tall_base * 8)
        for c in range(COLS):
            for cp in t_cp[c]:
                cp.wait()
            for g in range(plan.talls // 8):
                for row in range(24):
                    at = pl.ds(g * 8 * 24 + row, 8, stride=24)
                    v = advance_of(local[4][c, at, :], local[5][c, at, :])
                    put(row % 12, c, plan.tall_base + 16 * g + row // 12, 2, v)
        flush(1, plan.tall_base * 8, (plan.emb_base - plan.tall_base) * 8)
        for c in e_cp:
            c.wait()
        v = advance_of(local[6][...], local[7][...])
        for row in range(24):
            for c in range(COLS):
                sub, j = cell(row % 12, c)
                at = (plan.emb_base + row // 12) * 8 + sub
                z[j, at : at + 1, :] = v[row : row + 1, lanes(c)]
        tail = plan.sq_base + plan.half
        if tail < plan.devices:
            z[:, pl.ds(tail * 8, (plan.devices - tail) * 8), :] = jnp.zeros(
                (TILES, (plan.devices - tail) * 8, 128), F32
            )
        for r in range(6):
            for c in s_cp[r]:
                c.wait()

            @pl.loop(0, plan.half // 8)
            def _(g):
                for ab in range(2):
                    at = pl.ds(
                        pl.multiple_of(r * plan.squares + ab * plan.half + 8 * g, 8), 8
                    )
                    v = advance_of(local[0][at, :], local[1][at, :])
                    for c in range(COLS):
                        put(6 * ab + r, c, plan.sq_base + 8 * g, 1, v[:, lanes(c)])

        flush(2, plan.emb_base * 8, rows - plan.emb_base * 8)
        for c in copies:
            c.wait()

    any_spec = pl.BlockSpec(memory_space=pl.ANY)
    n_copies = 2 * (6 + COLS + 1 + 6)
    return pl.pallas_call(
        kernel,
        out_shape=jax.ShapeDtypeStruct((rows, LANES), BF16),
        in_specs=[any_spec] * 8,
        out_specs=any_spec,
        scratch_shapes=[
            pltpu.VMEM((COLS, a.shape[0], 128) if i in (4, 5) else a.shape, F32)
            for i, a in enumerate(arrays)
        ]
        + [
            pltpu.VMEM((TILES, rows, 128), F32),
            pltpu.VMEM((rows, LANES), BF16),
            pltpu.SemaphoreType.DMA((n_copies,)),
            pltpu.SemaphoreType.DMA((3,)),
        ],
        compiler_params=vmem_limit(),
        name="pack",
    )(*arrays)


def dot(x, y):
    return jnp.dot(x, y, preferred_element_type=F32)


def dot_nt(x, y):
    return lax.dot_general(x, y, (((1,), (1,)), ((), ())), preferred_element_type=F32)


def dot_tn(x, y):
    return lax.dot_general(x, y, (((0,), (0,)), ((), ())), preferred_element_type=F32)


def trace_of(gram):
    n = gram.shape[0]
    eye = lax.broadcasted_iota(jnp.int32, (128, 128), 0) == lax.broadcasted_iota(
        jnp.int32, (128, 128), 1
    )
    total = jnp.zeros((128, 128), F32)
    for b in range(n // 128):
        at = slice(128 * b, 128 * b + 128)
        total = total + jnp.where(eye, gram[at, at], 0.0)
    return jnp.sum(total)


def square_steps(x, g, p, y):
    gram = dot_nt(x[...], x[...])
    norm = jnp.full((1, 1), trace_of(gram), F32)
    s = 1.0 / (jnp.sqrt(norm) + EPSILON)
    g[...] = (gram * (s * s)).astype(BF16)
    p[...] = (B_COEF * g[...].astype(F32) + C_COEF * dot(g[...], g[...])).astype(BF16)
    x[...] = (s * (A_COEF * x[...].astype(F32) + dot(p[...], x[...]))).astype(BF16)
    for last in (False, True):
        g[...] = dot_nt(x[...], x[...]).astype(BF16)
        p[...] = (B_COEF * g[...].astype(F32) + C_COEF * dot(g[...], g[...])).astype(BF16)
        new = A_COEF * x[...].astype(F32) + dot(p[...], x[...])
        if last:
            y[...] = new
        else:
            x[...] = new.astype(BF16)


def gather_blocks(role, received, devices):
    def kernel(role_ref, in_ref, xa_ref, xb_ref, gram_ref, z):
        @pl.loop(0, devices // 8)
        def _(i):
            at = pl.ds(pl.multiple_of(i * 64, 64), 64)
            for j in range(TILES):
                z[j, at, :] = in_ref[at, lanes(j)].astype(F32)

        @pl.loop(0, devices // 16)
        def _(b):
            for k in range(12):
                ref = xa_ref if k < 6 else xb_ref
                to = pl.ds(pl.multiple_of((b * 6 + k % 6) * 16, 16), 16)
                for c in range(COLS):
                    sub, j = cell(k, c)
                    halves = [
                        z[j, pl.ds((2 * b + half) * 64 + sub, 8, stride=8), :]
                        for half in range(2)
                    ]
                    ref[to, lanes(c)] = jnp.concatenate(halves, 0).astype(BF16)

        @pl.when(role_ref[0] == 1)
        def _():
            gram_ref[...] = (
                dot_nt(xa_ref[...], xa_ref[...]) + dot_nt(xb_ref[...], xb_ref[...])
            ).astype(gram_ref.dtype)

        @pl.when(role_ref[0] == 2)
        def _():
            gram_ref[...] = (
                dot_tn(xa_ref[...], xa_ref[...]) + dot_tn(xb_ref[...], xb_ref[...])
            ).astype(gram_ref.dtype)

    vm = pl.BlockSpec(memory_space=pltpu.VMEM)
    block = jax.ShapeDtypeStruct((W, W), BF16)
    return pl.pallas_call(
        kernel,
        out_shape=(block, block, jax.ShapeDtypeStruct((W, W), F32)),
        in_specs=[pl.BlockSpec(memory_space=pltpu.SMEM), vm],
        out_specs=(vm, vm, vm),
        scratch_shapes=[pltpu.VMEM((TILES, devices * 8, 128), F32)],
        compiler_params=vmem_limit(),
        name="gather_blocks",
    )(role, received)


def first_square(role, xa):
    def kernel(role_ref, x_ref, y_ref, x, g, p):
        @pl.when(role_ref[0] == 0)
        def _():
            x[...] = x_ref[...]
            square_steps(x, g, p, y_ref)

    vm = pl.BlockSpec(memory_space=pltpu.VMEM)
    return pl.pallas_call(
        kernel,
        out_shape=jax.ShapeDtypeStruct((W, W), F32),
        in_specs=[pl.BlockSpec(memory_space=pltpu.SMEM), vm],
        out_specs=vm,
        scratch_shapes=[pltpu.VMEM((W, W), BF16)] * 3,
        compiler_params=vmem_limit(),
        cost_estimate=pl.CostEstimate(
            flops=18 * W**3, bytes_accessed=6 * W * W, transcendentals=0
        ),
        name="first_square",
    )(role, xa)


def finish(role, xa, xb, ya, gram, other_gram, devices):
    def kernel(role_ref, xa_ref, xb_ref, ya_ref, g1_ref, g2_ref, out_ref, x, g, p, t, q, ys, yt, z):
        def spread(k, source):
            @pl.loop(0, devices // 8)
            def _(i):
                at = ((i // 2) * 6 + k % 6) * 16 + (i % 2) * 8
                v = source[pl.ds(pl.multiple_of(at, 8), 8), :]
                for c in range(COLS):
                    sub, j = cell(k, c)
                    z[j, pl.ds(i * 64 + sub, 8, stride=8), :] = v[:, lanes(c)]

        @pl.when(role_ref[0] == 0)
        def _():
            for k in range(6):
                spread(k, ya_ref)
            x[...] = xb_ref[...]
            square_steps(x, g, p, yt)
            for k in range(6, 12):
                spread(k, yt)

        @pl.when(role_ref[0] > 0)
        def _():
            gram = g1_ref[...] + g2_ref[...]
            norm = jnp.full((1, 1), trace_of(gram), F32)
            s = 1.0 / (jnp.sqrt(norm) + EPSILON)
            g[...] = (gram * (s * s)).astype(BF16)
            p[...] = (B_COEF * g[...].astype(F32) + C_COEF * dot(g[...], g[...])).astype(BF16)
            t[...] = dot(p[...], g[...]).astype(BF16)
            x[...] = (
                A_COEF * A_COEF * g[...].astype(F32)
                + 2 * A_COEF * t[...].astype(F32)
                + dot(p[...], t[...])
            ).astype(BF16)
            q[...] = (B_COEF * x[...].astype(F32) + C_COEF * dot(x[...], x[...])).astype(BF16)
            t[...] = dot(q[...], x[...]).astype(BF16)
            g[...] = (
                A_COEF * A_COEF * x[...].astype(F32)
                + 2 * A_COEF * t[...].astype(F32)
                + dot(q[...], t[...])
            ).astype(BF16)
            x[...] = (
                A_COEF * p[...].astype(F32) + A_COEF * q[...].astype(F32) + dot(q[...], p[...])
            ).astype(BF16)
            t[...] = (B_COEF * g[...].astype(F32) + C_COEF * dot(g[...], g[...])).astype(BF16)
            q[...] = (
                A_COEF * x[...].astype(F32)
                + A_COEF * A_COEF * t[...].astype(F32)
                + dot(t[...], x[...])
            ).astype(BF16)
            cube = A_COEF**3

            @pl.when(role_ref[0] == 1)
            def _():
                ys[...] = s * (cube * xa_ref[...].astype(F32) + dot(q[...], xa_ref[...]))
                yt[...] = s * (cube * xb_ref[...].astype(F32) + dot(q[...], xb_ref[...]))

            @pl.when(role_ref[0] == 2)
            def _():
                ys[...] = s * (cube * xa_ref[...].astype(F32) + dot(xa_ref[...], q[...]))
                yt[...] = s * (cube * xb_ref[...].astype(F32) + dot(xb_ref[...], q[...]))

            for k in range(12):
                spread(k, ys if k < 6 else yt)

        @pl.loop(0, devices // 8)
        def _(i):
            at = pl.ds(pl.multiple_of(i * 64, 64), 64)
            for j in range(TILES):
                out_ref[at, lanes(j)] = z[j, at, :].astype(BF16)

    vm = pl.BlockSpec(memory_space=pltpu.VMEM)
    return pl.pallas_call(
        kernel,
        out_shape=jax.ShapeDtypeStruct((devices * 8, LANES), BF16),
        in_specs=[pl.BlockSpec(memory_space=pltpu.SMEM)] + [vm] * 5,
        out_specs=vm,
        scratch_shapes=[pltpu.VMEM((W, W), BF16)] * 5
        + [pltpu.VMEM((W, W), F32)] * 2
        + [pltpu.VMEM((TILES, devices * 8, 128), F32)],
        compiler_params=vmem_limit(),
        name="finish",
    )(role, xa, xb, ya, gram, other_gram)


def unpack(plan, returned, sq_w, wide_w, tall_w, emb_w):
    rows = plan.devices * 8
    weights = (sq_w, wide_w, tall_w, emb_w)
    scales = (math.sqrt(W), math.sqrt(4 * W), math.sqrt(4 * W), math.sqrt(4 * W))

    def kernel(*refs):
        ret = refs[0]
        w_hbm = refs[1:5]
        d_hbm = refs[5:9]
        n_hbm = refs[9:13]
        w_v = refs[13:17]
        d_v = refs[17:21]
        n_v = refs[21:25]
        rb, z, in_sems, out_sems = refs[25:29]
        spans = (
            (0, plan.tall_base * 8),
            (plan.tall_base * 8, plan.emb_base * 8),
            (plan.emb_base * 8, (plan.sq_base + plan.half) * 8),
        )
        r_cp = []
        for i, (lo, hi) in enumerate(spans):
            c = pltpu.make_async_copy(
                ret.at[pl.ds(lo, hi - lo)], rb.at[pl.ds(lo, hi - lo)], in_sems.at[i]
            )
            c.start()
            r_cp.append(c)
        w_cp = [None] * 4
        t_cp = []
        for j, i in enumerate((1, 3, 0)):
            w_cp[i] = pltpu.make_async_copy(w_hbm[i], w_v[i], in_sems.at[3 + j])
            w_cp[i].start()
        for c in range(COLS):
            t_cp.append(
                pltpu.make_async_copy(w_hbm[2].at[:, lanes(c)], w_v[2].at[c], in_sems.at[6 + c])
            )
            t_cp[c].start()
        out = []

        def send_out(i, start, size):
            for hbm, local in ((d_hbm[i], d_v[i]), (n_hbm[i], n_v[i])):
                if i == 2:
                    ends = local.at[start], hbm.at[:, lanes(start)]
                else:
                    ends = local.at[pl.ds(start, size)], hbm.at[pl.ds(start, size)]
                c = pltpu.make_async_copy(*ends, out_sems.at[len(out)])
                c.start()
                out.append(c)

        def take(k, c, dest0, step):
            sub, j = cell(k, c)
            return z[j, pl.ds(dest0 * 8 + sub, 8, stride=8 * step), :]

        def place(i, at, v):
            w = w_v[i][at]
            d = scales[i] * v
            d_v[i][at] = d
            n_v[i][at] = w - STEP_RATE * (d + WEIGHT_DECAY * w)

        def widen(lo, hi):
            for j in range(TILES):
                z[j, pl.ds(lo, hi - lo), :] = rb[pl.ds(lo, hi - lo), lanes(j)].astype(F32)

        r_cp[0].wait()
        widen(*spans[0])
        w_cp[1].wait()
        for r in range(6):
            for g in range(plan.wides // 8):
                at = pl.ds(r * plan.wides + 8 * g, 8)
                for h in range(2):
                    for ab in range(2):
                        for c in range(COLS):
                            v = take(6 * ab + r, c, 16 * g + h, 2)
                            place(1, (at, lanes((2 * h + ab) * COLS + c)), v)
            send_out(1, r * plan.wides, plan.wides)
        r_cp[1].wait()
        widen(*spans[1])
        for c in range(COLS):
            t_cp[c].wait()
            for g in range(plan.talls // 8):
                for row in range(24):
                    at = pl.ds(g * 8 * 24 + row, 8, stride=24)
                    v = take(row % 12, c, plan.tall_base + 16 * g + row // 12, 2)
                    place(2, (c, at, slice(None)), v)
            send_out(2, c, None)
        r_cp[2].wait()
        widen(*spans[2])
        w_cp[3].wait()
        for row in range(24):
            for c in range(COLS):
                sub, j = cell(row % 12, c)
                at = (plan.emb_base + row // 12) * 8 + sub
                place(3, (slice(row, row + 1), lanes(c)), z[j, at : at + 1, :])
        send_out(3, 0, 24)
        w_cp[0].wait()
        for r in range(6):

            @pl.loop(0, plan.half // 8)
            def _(g):
                for ab in range(2):
                    at = pl.ds(
                        pl.multiple_of(r * plan.squares + ab * plan.half + 8 * g, 8), 8
                    )
                    for c in range(COLS):
                        v = take(6 * ab + r, c, plan.sq_base + 8 * g, 1)
                        place(0, (at, lanes(c)), v)

            send_out(0, r * plan.squares, plan.squares)
        for c in out:
            c.wait()

    any_spec = pl.BlockSpec(memory_space=pl.ANY)
    shapes = [jax.ShapeDtypeStruct(w.shape, F32) for w in weights]
    n_out = 2 * (6 + COLS + 1 + 6)
    return pl.pallas_call(
        kernel,
        out_shape=shapes * 2,
        in_specs=[any_spec] * 5,
        out_specs=[any_spec] * 8,
        scratch_shapes=[
            pltpu.VMEM((COLS, w.shape[0], 128) if i == 2 else w.shape, F32)
            for i, w in enumerate(weights)
        ]
        * 3
        + [
            pltpu.VMEM((rows, LANES), BF16),
            pltpu.VMEM((TILES, rows, 128), F32),
            pltpu.SemaphoreType.DMA((6 + COLS,)),
            pltpu.SemaphoreType.DMA((n_out,)),
        ],
        compiler_params=vmem_limit(),
        name="unpack",
    )(returned, *weights)


def by_row(x):
    return jnp.transpose(x, (1, 0, 2)).reshape(-1, x.shape[2])


def by_matrix(x, shape):
    return jnp.transpose(x.reshape(shape[1], shape[0], shape[2]), (1, 0, 2))


def on_device(
    sq_grad,
    sq_moment,
    sq_weight,
    in_grad,
    in_moment,
    in_weight,
    out_grad,
    out_moment,
    out_weight,
    emb_grad,
    emb_moment,
    emb_weight,
):
    devices = lax.axis_size(AXES)
    me = lax.axis_index(AXES)
    plan = Plan(sq_grad.shape[0], in_grad.shape[0], out_grad.shape[0], devices)
    send = pack(
        plan,
        (by_row(sq_grad), by_row(sq_moment)),
        (by_row(in_grad), by_row(in_moment)),
        (out_grad.reshape(-1, W), out_moment.reshape(-1, W)),
        (emb_grad, emb_moment),
    )
    received = lax.all_to_all(send, AXES, split_axis=0, concat_axis=0, tiled=True)
    role = jnp.where(
        me < plan.tall_base,
        1,
        jnp.where(me < plan.sq_base, 2, jnp.where(me < plan.sq_base + plan.half, 0, -1)),
    )
    role = role.astype(jnp.int32).reshape(1)
    xa, xb, gram = gather_blocks(role, received, devices)
    other_gram = lax.ppermute(gram, AXES, [(i, i ^ 1) for i in range(devices)])
    ya = first_square(role, xa)
    result = finish(role, xa, xb, ya, gram, other_gram, devices)
    returned = lax.all_to_all(result, AXES, split_axis=0, concat_axis=0, tiled=True)
    new = unpack(
        plan,
        returned,
        by_row(sq_weight),
        by_row(in_weight),
        out_weight.reshape(-1, W),
        emb_weight,
    )
    sq_d, in_d, out_d, emb_d, sq_w, in_w, out_w, emb_w = new
    return (
        MOMENTUM_DECAY * sq_moment + sq_grad,
        by_matrix(sq_w, sq_weight.shape),
        by_matrix(sq_d, sq_weight.shape),
        MOMENTUM_DECAY * in_moment + in_grad,
        by_matrix(in_w, in_weight.shape),
        by_matrix(in_d, in_weight.shape),
        MOMENTUM_DECAY * out_moment + out_grad,
        out_w.reshape(out_weight.shape),
        out_d.reshape(out_weight.shape),
        MOMENTUM_DECAY * emb_moment + emb_grad,
        emb_w,
        emb_d,
    )


def solution(mesh):
    matrix = P(None, AXES, None)
    table = P(AXES, None)
    specs = (matrix,) * 9 + (table,) * 3
    return jax.shard_map(
        on_device, mesh=mesh, in_specs=specs, out_specs=specs, check_vma=False
    )
```
